256 devices in a mesh: win: 16 (over z, x_lo), frm: 16 (over x_hi, y, core).
Axes of the slice: x: 4 (x_hi: 2, x_lo: 2; x = x_hi * 2 + x_lo), y: 4, z: 8, core: 2. Of those that a mesh axis runs over, the one named last changes fastest.
Arguments:
- hidden_state: bfloat16 [65536, 1536], P(('win', 'frm')), may hold values from -600 to 600
- latent: float32 [65536, 64], P(('win', 'frm')), may hold values from -6 to 6
- stale_kv: bfloat16 [65536, 1536], P(('win', 'frm')), may hold values from -100 to 100
- mod_shift: float32 [16, 1536], P('win'), may hold values from -3 to 3
- mod_scale: float32 [16, 1536], P('win'), may hold values from -3 to 3
- mod_gate: float32 [16, 1536], P('win'), may hold values from 0.5 to 4
- w_query: bfloat16 [1536, 768], replicated, may hold values from -0.29882812 to 0.29882812
- w_keyval: bfloat16 [1536, 1536], replicated, may hold values from -0.15625 to 0.15625
- w_out: bfloat16 [768, 1536], replicated, may hold values from -0.21875 to 0.21875
- w_final: bfloat16 [1536, 64], replicated, may hold values from -0.15625 to 0.15625
- step_size: float32 [16], P('win'), may hold values from 0.5 to 1.5
Outputs:
- next_latent: float32 [65536, 64], P(('win', 'frm'))
The draws below stay inside these ranges and needn't reach their ends.
All inputs are finite; a program needn't handle non-finite values.
Results may differ from the reference program's by a relative error of at most 0.0024.
Values may be sent and summed in bfloat16 or wider, within the bound.
No kernel may reach another device: no remote copies, remote signals or barrier semaphores. Data moves between devices by JAX's collectives and lax.ppermute only.
A program may use at most 192 MiB of HBM per device.

```python
import math
import jax
import jax.numpy as jnp
from jax import lax

D = 1536
HEADS = 12
HEAD_DIM = 64
CH = 64
F_DEV = 256
QW = 768
FRAMES = 4096
SEAM = 2048
WINS = 16
N_FRM = 16


def draw_hidden_state(key, part):
    noise_key, column_key = jax.random.split(key, 2)
    total_rows = WINS * FRAMES
    values = jnp.clip(jax.random.normal(noise_key, (total_rows, D), jnp.float32), -6.0, 6.0)
    column_scale = jnp.exp(jax.random.uniform(column_key, (1, D), jnp.float32, 0.0, math.log(10.0)))
    values = values * column_scale
    return values.astype(jnp.bfloat16)


def draw_stale_kv(key, part):
    noise_key = jax.random.fold_in(key, 0)
    total_rows = WINS * FRAMES
    query_width = HEADS * HEAD_DIM
    values = jnp.clip(jax.random.normal(noise_key, (total_rows, 2 * query_width), jnp.float32), -6.0, 6.0)
    return values.astype(jnp.bfloat16)


def shard_levels(rng, dims, cuts, least, top_value):
    gain = 1.0
    for position, blocks in cuts:
        draws = jax.random.uniform(jax.random.fold_in(jax.random.fold_in(rng, 6), position), (blocks,), jnp.float32, least / len(cuts), top_value / len(cuts))
        gain = gain * jnp.repeat(jnp.exp(draws), dims[position] // blocks).reshape((-1,) + (1,) * (len(dims) - 1 - position))
    return gain


def normal_values(stream_key, dims, spread, limit, shards=(), kind=jnp.bfloat16):
    drawn = spread * jax.random.normal(stream_key, dims, jnp.float32)
    if shards:
        drawn = drawn * shard_levels(stream_key, dims, shards, -0.22, 0.18)
    return jnp.clip(drawn, -limit, limit).astype(kind)


def setup_inputs(seed: int = 0) -> dict:
    keys = jax.random.split(jax.random.key(seed), 12)
    return {
        "hidden_state": draw_hidden_state(jax.random.fold_in(keys[11], 71), 0),
        "latent": normal_values(keys[1], (WINS * FRAMES, CH), 1.0, 6.0, ((0, 256),), jnp.float32),
        "stale_kv": draw_stale_kv(jax.random.fold_in(keys[11], 71), 0),
        "mod_shift": normal_values(keys[3], (WINS, D), 0.5, 3.0, ((0, 16),), jnp.float32),
        "mod_scale": normal_values(keys[4], (WINS, D), 0.5, 3.0, ((0, 16),), jnp.float32),
        "mod_gate": jnp.clip(jnp.exp(math.log(4.0) - 2.0794415 * jax.random.uniform(keys[5], (WINS, D), jnp.float32) ** shard_levels(keys[5], (WINS, D), ((0, 16),), -0.2, 0.2)), 0.5, 4.0),
        "w_query": normal_values(keys[6], (D, QW), 0.05, 0.29882812),
        "w_keyval": normal_values(keys[7], (D, 2 * QW), D ** -0.5, 0.15625),
        "w_out": normal_values(keys[8], (QW, D), QW ** -0.5, 0.21875),
        "w_final": normal_values(keys[9], (D, CH), D ** -0.5, 0.15625),
        "step_size": jnp.clip(0.5 + 1.0 * jax.random.uniform(keys[10], (WINS,), jnp.float32) ** shard_levels(keys[10], (WINS,), ((0, 16),), -0.2, 0.2), 0.5, 1.5),
    }


def layer_norm(values):
    average = lax.optimization_barrier(jnp.mean(values, axis=-1, keepdims=True))
    centred = values - average
    variance = lax.optimization_barrier(jnp.mean(centred * centred, axis=-1, keepdims=True))
    return centred * lax.rsqrt(variance + 1e-06)

def reference(hidden_state, latent, stale_kv, mod_shift, mod_scale, mod_gate, w_query, w_keyval, w_out, w_final, step_size):
    query_width = HEADS * HEAD_DIM
    scale_factor = HEAD_DIM ** (-0.5)

    def window_update(inputs):
        window_hidden, window_latent, window_kv, shift_row, scale_row, gate_row, window_step = inputs
        stream = window_hidden.astype(jnp.float32)
        modulated = (layer_norm(stream) * (1.0 + scale_row) + shift_row).astype(jnp.bfloat16)
        queries = jnp.dot(modulated, w_query, preferred_element_type=jnp.float32).astype(jnp.bfloat16)
        fresh_kv = jnp.dot(modulated, w_keyval, preferred_element_type=jnp.float32).astype(jnp.bfloat16)

        def frame_block(block_id):
            block_start = (block_id * F_DEV).astype(jnp.int32)
            fresh_rows = lax.dynamic_slice_in_dim(fresh_kv, block_start, F_DEV, 0)
            key_value = lax.dynamic_update_slice_in_dim(window_kv, fresh_rows, block_start, 0)
            query_heads = lax.dynamic_slice_in_dim(queries, block_start, F_DEV, 0)
            query_heads = query_heads.reshape(F_DEV, HEADS, HEAD_DIM).astype(jnp.float32)
            key_rows = key_value[:, :query_width].reshape(FRAMES, HEADS, HEAD_DIM).astype(jnp.float32)
            value_rows = key_value[:, query_width:].reshape(FRAMES, HEADS, HEAD_DIM).astype(jnp.float32)
            scores = jnp.einsum('qhd,khd->hqk', query_heads, key_rows) * scale_factor
            row_max = lax.optimization_barrier(jnp.max(scores, axis=-1, keepdims=True))
            probs = jnp.exp(scores - row_max)
            totals = lax.optimization_barrier(jnp.sum(probs, axis=-1))
            weights = lax.optimization_barrier(probs.astype(jnp.bfloat16)).astype(jnp.float32)
            summed = jnp.einsum('hqk,khd->qhd', weights, value_rows)
            attended = summed / jnp.transpose(totals)[:, :, None]
            return attended.reshape(F_DEV, query_width).astype(jnp.bfloat16)
        attention = lax.map(frame_block, jnp.arange(N_FRM, dtype=jnp.int32)).reshape(FRAMES, query_width)
        combined = stream + gate_row * jnp.dot(attention, w_out, preferred_element_type=jnp.float32)
        normed = layer_norm(combined).astype(jnp.bfloat16)
        velocity = jnp.dot(normed, w_final, preferred_element_type=jnp.float32)
        return window_latent + window_step * velocity
    advanced = lax.map(window_update, (hidden_state.reshape(WINS, FRAMES, D), latent.reshape(WINS, FRAMES, CH), stale_kv.reshape(WINS, FRAMES, 2 * query_width), mod_shift, mod_scale, mod_gate, step_size))
    ramp_up = ((jnp.arange(SEAM, dtype=jnp.float32) + 0.5) / SEAM)[:, None]
    tail_rows = advanced[:-1, FRAMES - SEAM:]
    head_rows = advanced[1:, :SEAM]
    blended = (1.0 - ramp_up) * tail_rows + ramp_up * head_rows
    advanced = advanced.at[:-1, FRAMES - SEAM:].set(blended)
    advanced = advanced.at[1:, :SEAM].set(blended)
    return advanced.reshape(WINS * FRAMES, CH)
```

```python
import functools

import jax
import jax.numpy as jnp
from jax import lax
from jax.experimental import pallas as pl
from jax.experimental.pallas import tpu as pltpu
from jax.sharding import PartitionSpec as P

HEADS = 12
HEAD_DIM = 64
BLK = 256
D = 1536
HALF = 384
PAIRS = 3
LOG2E = 1.4426950408889634
F32 = jnp.float32
BF16 = jnp.bfloat16


def flip_x(i):
    return i ^ 8


def flip_core(i):
    return i ^ 1


def step_y(by):
    def to(i):
        x, y, c = i // 8, (i // 2) % 4, i % 2
        return x * 8 + ((y + by) % 4) * 2 + c

    return to


def send(value, to):
    return lax.ppermute(value, "frm", [(i, to(i)) for i in range(16)])


def normalise(values):
    average = jnp.mean(values, axis=-1, keepdims=True)
    centred = values - average
    variance = jnp.mean(centred * centred, axis=-1, keepdims=True)
    return centred * lax.rsqrt(variance + 1e-06)


def query_kernel(sel, hidden, shift, scale, w, q_send, q_own, modulated):
    step = pl.program_id(0)

    @pl.when(step == 0)
    def _():
        x = normalise(hidden[...].astype(F32))
        modulated[...] = (x * (1.0 + scale[...]) + shift[...]).astype(BF16)

    q = jnp.dot(modulated[...], w[...], preferred_element_type=F32).astype(BF16)
    q = q * jnp.asarray(HEAD_DIM**-0.5, BF16)

    @pl.when(step == 0)
    def _():
        q_send[...] = q

    @pl.when(step == 1)
    def _():
        q_own[...] = q


def make_queries(sel, hidden, shift, scale, w_query):
    whole = lambda s: pl.BlockSpec(s, lambda i, sel: (0, 0))
    return pl.pallas_call(
        query_kernel,
        grid_spec=pltpu.PrefetchScalarGridSpec(
            num_scalar_prefetch=1,
            grid=(2,),
            in_specs=[
                whole((BLK, D)),
                whole((1, D)),
                whole((1, D)),
                pl.BlockSpec((D, HALF), lambda i, sel: (0, sel[i])),
            ],
            out_specs=[whole((BLK, HALF)), whole((BLK, HALF)), whole((BLK, D))],
        ),
        out_shape=[
            jax.ShapeDtypeStruct((BLK, HALF), BF16),
            jax.ShapeDtypeStruct((BLK, HALF), BF16),
            jax.ShapeDtypeStruct((BLK, D), BF16),
        ],
        name="queries",
    )(sel, hidden, shift, scale, w_query)


def fresh_kernel(sel, modulated, w, f_send, f_own):
    step = pl.program_id(0)
    kv = jnp.dot(modulated[...], w[...], preferred_element_type=F32).astype(BF16)
    for i in range(4):
        out = (f_send, f_own)[i // 2]

        @pl.when(step == i)
        def _(out=out, i=i):
            out[:, (i % 2) * HALF : (i % 2 + 1) * HALF] = kv


def make_fresh(sel, modulated, w_keyval):
    whole = lambda s: pl.BlockSpec(s, lambda i, sel: (0, 0))
    return pl.pallas_call(
        fresh_kernel,
        grid_spec=pltpu.PrefetchScalarGridSpec(
            num_scalar_prefetch=1,
            grid=(4,),
            in_specs=[
                whole((BLK, D)),
                pl.BlockSpec((D, HALF), lambda i, sel: (0, sel[i // 2] + 2 * (i % 2))),
            ],
            out_specs=[whole((BLK, 2 * HALF)), whole((BLK, 2 * HALF))],
        ),
        out_shape=[jax.ShapeDtypeStruct((BLK, 2 * HALF), BF16)] * 2,
        name="fresh",
    )(sel, modulated, w_keyval)


def attend_kernel(*refs, lists, n_keys, first, last):
    n_q = len(lists)
    qs = refs[:n_q]
    keys = refs[n_q : n_q + n_keys]
    values = refs[n_q + n_keys : n_q + 2 * n_keys]
    rest = refs[n_q + 2 * n_keys :]
    if not first:
        acc_in, max_in = rest[0], rest[1]
        rest = rest[2:]
    lower = lax.broadcasted_iota(jnp.int32, (BLK, 128), 1) < HEAD_DIM
    for j in range(n_q):
        q = qs[j][...]
        accs, maxs = [], []
        for h in range(2):
            mine = lower if h == 0 else jnp.logical_not(lower)
            qh = jnp.where(mine, q, jnp.zeros_like(q))
            if first:
                acc = top = None
            else:
                acc = acc_in[j, h]
                top = max_in[j, 0][:, h * HEAD_DIM : h * HEAD_DIM + 1]
            for i in lists[j]:
                rows = keys[i].shape[0]
                s = lax.dot_general(
                    qh, keys[i][...], (((1,), (1,)), ((), ())), preferred_element_type=F32
                )
                new = jnp.max(s, axis=-1, keepdims=True)
                if top is not None:
                    new = jnp.maximum(top, new)
                p = jnp.exp2((s - new) * LOG2E).astype(BF16)
                v = values[i][...]
                v = jnp.where(mine[:rows], v, jnp.ones_like(v))
                o = jnp.dot(p, v, preferred_element_type=F32)
                acc = o if top is None else acc * jnp.exp2((top - new) * LOG2E) + o
                top = new
            accs.append(acc)
            maxs.append(top)
        if last:
            top = jnp.where(lower, accs[0], accs[1])
            total = pltpu.roll(jnp.where(lower, accs[1], accs[0]), HEAD_DIM, 1)
            rest[j][...] = (top / total).astype(BF16)
        else:
            rest[0][j, 0], rest[0][j, 1] = accs
            rest[1][j, 0] = jnp.where(lower, maxs[0], maxs[1])


def attend(qs, lists, arrays, state, last, which, name):
    first = state is None
    n_q = len(qs)
    rows = [a.shape[0] for a in arrays]
    q_spec = pl.BlockSpec((BLK, 128), lambda p: (0, p))
    acc_spec = pl.BlockSpec((n_q, 2, BLK, 128), lambda p: (which, p, 0, 0))
    max_spec = pl.BlockSpec((n_q, 1, BLK, 128), lambda p: (which, p, 0, 0))
    in_specs = [q_spec] * n_q
    in_specs += [pl.BlockSpec((r, 128), lambda p: (0, p)) for r in rows]
    in_specs += [pl.BlockSpec((r, 128), lambda p: (0, p + PAIRS)) for r in rows]
    args = list(qs) + list(arrays) + list(arrays)
    if not first:
        in_specs += [acc_spec, max_spec]
        args += list(state)
    if last:
        out_specs = [q_spec] * n_q
        out_shape = [jax.ShapeDtypeStruct((BLK, HALF), BF16)] * n_q
    else:
        out_specs = [acc_spec, max_spec]
        out_shape = [
            jax.ShapeDtypeStruct((2, 2 * PAIRS, BLK, 128), F32),
            jax.ShapeDtypeStruct((2, PAIRS, BLK, 128), F32),
        ]
    return pl.pallas_call(
        functools.partial(
            attend_kernel, lists=lists, n_keys=len(arrays), first=first, last=last
        ),
        grid=(PAIRS,),
        in_specs=in_specs,
        out_specs=out_specs,
        out_shape=out_shape,
        name=name,
    )(*args)


def finish_kernel(
    step, o_own, o_other, w_own, w_other, hidden, gate, w_final, latent, advanced
):
    mixed = jnp.dot(o_own[...], w_own[...], preferred_element_type=F32)
    mixed += jnp.dot(o_other[...], w_other[...], preferred_element_type=F32)
    combined = hidden[...].astype(F32) + gate[...] * mixed
    normed = normalise(combined).astype(BF16)
    velocity = jnp.dot(normed, w_final[...], preferred_element_type=F32)
    advanced[...] = latent[...] + step[0] * velocity


def finish(sel, o_own, o_other, w_out, hidden, gate, w_final, latent, step_size):
    whole = lambda s: pl.BlockSpec(s, lambda i, sel: (0, 0))
    return pl.pallas_call(
        lambda sel, *refs: finish_kernel(*refs),
        grid_spec=pltpu.PrefetchScalarGridSpec(
            num_scalar_prefetch=1,
            grid=(1,),
            in_specs=[
                pl.BlockSpec(memory_space=pltpu.SMEM),
                whole((BLK, HALF)),
                whole((BLK, HALF)),
                pl.BlockSpec((HALF, D), lambda i, sel: (sel[1], 0)),
                pl.BlockSpec((HALF, D), lambda i, sel: (sel[0], 0)),
                whole((BLK, D)),
                whole((1, D)),
                whole((D, 64)),
                whole((BLK, 64)),
            ],
            out_specs=[whole((BLK, 64))],
        ),
        out_shape=[jax.ShapeDtypeStruct((BLK, 64), F32)],
        name="finish",
    )(sel, step_size, o_own, o_other, w_out, w_out, hidden, gate, w_final, latent)[0]


def on_device(
    hidden_state,
    latent,
    stale_kv,
    mod_shift,
    mod_scale,
    mod_gate,
    w_query,
    w_keyval,
    w_out,
    w_final,
    step_size,
):
    frame_id = lax.axis_index("frm")
    window_id = lax.axis_index("win")
    frame_devs = lax.axis_size("frm")
    window_devs = lax.axis_size("win")
    side = frame_id // 8
    sel = jnp.stack([1 - side, side]).astype(jnp.int32)

    k0, k1, v0, v1 = (stale_kv[:, i * HALF : (i + 1) * HALF] for i in range(4))
    low = jnp.concatenate([k0, v0], axis=1)
    high = jnp.concatenate([k1, v1], axis=1)
    a_own = jnp.where(side == 0, low, high)
    a_send = jnp.where(side == 0, high, low)

    c_own = send(a_send, flip_x)
    a_prev = send(a_own, step_y(1))
    a_next = send(a_own, step_y(-1))
    b_own = send(a_own, flip_core)

    q_send, q_own, modulated = make_queries(sel, hidden_state, mod_shift, mod_scale, w_query)
    q_opp = send(q_send, flip_x)
    f_send, f_own = make_fresh(sel, modulated, w_keyval)
    f_opp = send(f_send, flip_x)

    h = BLK // 2
    b_prev = send(a_prev, flip_core)
    b_next = send(a_next, flip_core)
    a_far0 = send(a_prev[:h], step_y(1))
    a_far1 = send(a_next[h:], step_y(-1))
    b_far0 = send(a_far0, flip_core)
    b_far1 = send(a_far1, flip_core)

    d_own = send(c_own, flip_core)
    c_prev = send(c_own, step_y(1))
    c_next = send(c_own, step_y(-1))
    d_prev = send(c_prev, flip_core)
    d_next = send(c_next, flip_core)
    c_far0 = send(c_prev[:h], step_y(1))
    c_far1 = send(c_next[h:], step_y(-1))
    d_far0 = send(c_far0, flip_core)
    d_far1 = send(c_far1, flip_core)

    qs = [q_own, q_opp]
    four = [[0, 1, 2, 3]] * 2
    state = attend(qs, four, [a_prev, a_next, b_prev, b_next], None, False, 0, "near")
    local = [[0, 2, 3, 5], [1, 2, 4, 5]]
    state = attend(
        qs, local, [f_own, a_own, b_own, c_own, f_opp, d_own], state, False, 0, "local"
    )
    state = attend(qs, four, [a_far0, a_far1, b_far0, b_far1], state, False, 0, "far")
    state = attend(qs, four, [c_prev, c_next, d_prev, d_next], state, False, 0, "near2")
    o_own, o_send = attend(
        qs, four, [c_far0, c_far1, d_far0, d_far1], state, True, 0, "far2"
    )
    o_other = send(o_send, flip_x)
    advanced = finish(
        sel, o_own, o_other, w_out, hidden_state, mod_gate, w_final, latent, step_size
    )

    half = frame_devs // 2
    route = []
    for w in range(window_devs):
        for f in range(frame_devs):
            to_w, to_f = (w + 1, f - half) if f >= half else (w - 1, f + half)
            if 0 <= to_w < window_devs:
                route.append((w * frame_devs + f, to_w * frame_devs + to_f))
    partner = lax.ppermute(advanced, ("win", "frm"), route)
    seam = BLK * half
    in_tail = frame_id >= half
    pos = (lax.rem(frame_id, half) * BLK + jnp.arange(BLK, dtype=jnp.int32)).astype(F32)
    ramp = ((pos + 0.5) / seam)[:, None]
    met = jnp.where(in_tail, window_id < window_devs - 1, window_id > 0)
    mine = jnp.where(in_tail, 1.0 - ramp, ramp)
    theirs = jnp.where(in_tail, ramp, 1.0 - ramp)
    return jnp.where(met, mine * advanced + theirs * partner, advanced)


def solution(mesh):
    placed = (
        P(("win", "frm"), None),
        P(("win", "frm"), None),
        P(("win", "frm"), None),
        P("win", None),
        P("win", None),
        P("win", None),
        P(),
        P(),
        P(),
        P(),
        P("win"),
    )
    return jax.shard_map(
        on_device, mesh=mesh, in_specs=placed, out_specs=P(("win", "frm"), None), check_vma=False
    )
```

```python
import functools

import jax
import jax.numpy as jnp
from jax import lax
from jax.experimental import pallas as pl
from jax.experimental.pallas import tpu as pltpu
from jax.sharding import PartitionSpec as P

HEAD_DIM = 64
BLK = 256
D = 1536
HALF = 384
PAIRS = 3
LOG2E = 1.4426950408889634
F32 = jnp.float32
BF16 = jnp.bfloat16
VMEM = pl.BlockSpec(memory_space=pltpu.VMEM)
HBM = pl.BlockSpec(memory_space=pltpu.HBM)


def flip_x(i):
    return i ^ 8


def flip_core(i):
    return i ^ 1


def step_y(by):
    def to(i):
        x, y, c = i // 8, (i // 2) % 4, i % 2
        return x * 8 + ((y + by) % 4) * 2 + c

    return to


def send(value, to):
    return lax.ppermute(value, "frm", [(i, to(i)) for i in range(16)])


def kernel(body, out_shape, args, hbm=0, mib=16, **kw):
    many = isinstance(out_shape, list)
    cut = len(args) - hbm
    far = [pltpu.with_memory_space_constraint(a, pltpu.HBM) for a in args[cut:]]
    return pl.pallas_call(
        body,
        in_specs=[VMEM] * cut + [HBM] * hbm,
        out_specs=[VMEM] * len(out_shape) if many else VMEM,
        out_shape=out_shape,
        compiler_params=pltpu.CompilerParams(vmem_limit_bytes=mib << 20),
        **kw,
    )(*args[:cut], *far)


def struct(shape, dtype):
    return jax.ShapeDtypeStruct(shape, dtype)


def normalise(values):
    average = jnp.mean(values, axis=-1, keepdims=True)
    centred = values - average
    variance = jnp.mean(centred * centred, axis=-1, keepdims=True)
    return centred * lax.rsqrt(variance + 1e-06)


def upper():
    return lax.axis_index("frm") >= lax.axis_size("frm") // 2


def start_kernel(stale, a_own, a_send, sems):
    def halves(own):
        copies = []
        for i, (out, half) in enumerate([(a_send, 1 - own), (a_own, own)]):
            for j in range(2):
                cols = slice((2 * j + half) * HALF, (2 * j + half + 1) * HALF)
                to = out.at[:, j * HALF : (j + 1) * HALF]
                copies.append(pltpu.make_async_copy(stale.at[:, cols], to, sems.at[2 * i + j]))
        for c in copies:
            c.start()
        for c in copies:
            c.wait()

    @pl.when(upper())
    def _():
        halves(1)

    @pl.when(jnp.logical_not(upper()))
    def _():
        halves(0)


def query_kernel(*refs):
    sources, (q_send, q_own, modulated), buffers, sems = refs[:4], refs[4:7], refs[7:11], refs[11]
    hidden, shift, scale, w = buffers
    copies = [
        pltpu.make_async_copy(source, buffer, sems.at[i])
        for i, (source, buffer) in enumerate(zip(sources, buffers))
    ]
    for c in copies:
        c.start()
    for c in copies[:3]:
        c.wait()
    x = normalise(hidden[...].astype(F32))
    modulated[...] = (x * (1.0 + scale[...]) + shift[...]).astype(BF16)
    copies[3].wait()
    q = jnp.dot(modulated[...], w[...], preferred_element_type=F32).astype(BF16)
    q = q * jnp.asarray(HEAD_DIM**-0.5, BF16)

    @pl.when(jnp.logical_not(upper()))
    def _():
        q_own[...], q_send[...] = q[:, :HALF], q[:, HALF:]

    @pl.when(upper())
    def _():
        q_send[...], q_own[...] = q[:, :HALF], q[:, HALF:]


def fresh_kernel(modulated, step, source, f_send, f_own, step_row, w, sems):
    step_row[...] = jnp.broadcast_to(step[...].reshape(1, 1), step_row.shape)
    spans = [slice(i * 2 * HALF, (i + 1) * 2 * HALF) for i in range(2)]
    copies = [
        pltpu.make_async_copy(source.at[:, cols], w.at[:, cols], sems.at[i])
        for i, cols in enumerate(spans)
    ]
    for c in copies:
        c.start()
    for i, cols in enumerate(spans):
        copies[i].wait()
        x = jnp.dot(modulated[...], w[:, cols], preferred_element_type=F32).astype(BF16)
        to = slice(i * HALF, (i + 1) * HALF)

        @pl.when(jnp.logical_not(upper()))
        def _():
            f_own[:, to], f_send[:, to] = x[:, :HALF], x[:, HALF:]

        @pl.when(upper())
        def _():
            f_send[:, to], f_own[:, to] = x[:, :HALF], x[:, HALF:]


def attend_kernel(q_ref, *refs, n_keys, first, last):
    kvs, rest = refs[:n_keys], refs[n_keys:]
    if not first:
        acc_in, max_in = rest[0], rest[1]
        rest = rest[2:]
    lower = lax.broadcasted_iota(jnp.int32, (BLK, 128), 1) < HEAD_DIM
    for p in range(PAIRS):
        k_cols = slice(p * 128, (p + 1) * 128)
        v_cols = slice(HALF + p * 128, HALF + (p + 1) * 128)
        q = q_ref[:, k_cols]
        accs, tops = [], []
        for h, mine in enumerate((lower, jnp.logical_not(lower))):
            qh = jnp.where(mine, q, jnp.zeros_like(q))
            acc = top = None
            if not first:
                acc = acc_in[2 * p + h]
                top = jnp.where(mine, max_in[p], -3.0e38)
                top = jnp.max(top, axis=-1, keepdims=True)
            for kv in kvs:
                s = lax.dot_general(
                    qh, kv[:, k_cols], (((1,), (1,)), ((), ())), preferred_element_type=F32
                )
                new = jnp.max(s, axis=-1, keepdims=True)
                if top is not None:
                    new = jnp.maximum(top, new)
                probs = jnp.exp2((s - new) * LOG2E).astype(BF16)
                v = kv[:, v_cols]
                v = jnp.where(mine, v, jnp.ones_like(v))
                o = jnp.dot(probs, v, preferred_element_type=F32)
                acc = o if top is None else acc * jnp.exp2((top - new) * LOG2E) + o
                top = new
            accs.append(acc)
            tops.append(top)
        if last:
            summed = jnp.where(lower, accs[0], accs[1])
            total = pltpu.roll(jnp.where(lower, accs[1], accs[0]), HEAD_DIM, 1)
            rest[0][:, k_cols] = (summed / total).astype(BF16)
        else:
            rest[0][2 * p], rest[0][2 * p + 1] = accs
            rest[1][p] = jnp.where(lower, tops[0], tops[1])


def attend(q, arrays, state=None, last=False):
    args = [q, *arrays, *(state or ())]
    kw = {}
    if last:
        out_shape = struct((BLK, HALF), BF16)
    else:
        out_shape = [
            struct((2 * PAIRS, BLK, 128), F32),
            struct((PAIRS, BLK, 128), F32),
        ]
        if state:
            kw["input_output_aliases"] = {len(args) - 2: 0, len(args) - 1: 1}
    body = functools.partial(
        attend_kernel, n_keys=len(arrays), first=not state, last=last
    )
    return kernel(body, out_shape, args, **kw)


def finish_kernel(
    o_own,
    o_other,
    w_out,
    hidden,
    gate,
    w_final,
    latent,
    step,
    advanced,
    mine,
    theirs,
):
    frames, windows = lax.axis_size("frm"), lax.axis_size("win")
    half = frames // 2
    frame, window = lax.axis_index("frm"), lax.axis_index("win")
    tail = frame >= half
    begin = jnp.where(tail, frame - half, frame) * BLK
    pos = (begin + lax.broadcasted_iota(jnp.int32, (1, BLK), 1)).astype(F32)
    ramp = (pos + 0.5) / (BLK * half)
    met = jnp.where(tail, window < windows - 1, window > 0)
    mine[...] = jnp.where(met, jnp.where(tail, 1.0 - ramp, ramp), 1.0)
    theirs[...] = jnp.where(met, jnp.where(tail, ramp, 1.0 - ramp), 0.0)

    own = pl.multiple_of(jnp.where(tail, HALF, 0), HALF)
    other = pl.multiple_of(HALF - own, HALF)
    mixed = jnp.dot(o_own[...], w_out[pl.ds(own, HALF), :], preferred_element_type=F32)
    mixed += jnp.dot(
        o_other[...], w_out[pl.ds(other, HALF), :], preferred_element_type=F32
    )
    combined = hidden[...].astype(F32) + gate[...] * mixed
    normed = normalise(combined).astype(BF16)
    velocity = lax.dot_general(
        w_final[...], normed, (((1,), (1,)), ((), ())), preferred_element_type=F32
    )
    advanced[...] = latent[...] + step[...] * velocity


def on_device(
    hidden_state,
    latent,
    stale_kv,
    mod_shift,
    mod_scale,
    mod_gate,
    w_query,
    w_keyval,
    w_out,
    w_final,
    step_size,
):
    frame_devs = lax.axis_size("frm")
    window_devs = lax.axis_size("win")
    half = frame_devs // 2
    half_kv = struct((BLK, 2 * HALF), BF16)
    half_q = struct((BLK, HALF), BF16)
    row = struct((1, BLK), F32)

    a_own, a_send = kernel(
        start_kernel,
        [half_kv, half_kv],
        [stale_kv],
        hbm=1,
        scratch_shapes=[pltpu.SemaphoreType.DMA((4,))],
    )
    c_own = send(a_send, flip_x)
    a_prev = send(a_own, step_y(1))
    a_next = send(a_own, step_y(-1))
    b_own = send(a_own, flip_core)

    q_send, q_own, modulated = kernel(
        query_kernel,
        [half_q, half_q, struct((BLK, D), BF16)],
        [hidden_state, mod_shift, mod_scale, w_query],
        hbm=4,
        scratch_shapes=[
            pltpu.VMEM((BLK, D), BF16),
            pltpu.VMEM((1, D), F32),
            pltpu.VMEM((1, D), F32),
            pltpu.VMEM(w_query.shape, BF16),
            pltpu.SemaphoreType.DMA((4,)),
        ],
    )
    q_opp = send(q_send, flip_x)
    f_send, f_own, step_row = kernel(
        fresh_kernel,
        [half_kv, half_kv, row],
        [modulated, step_size, w_keyval],
        hbm=1,
        scratch_shapes=[pltpu.VMEM(w_keyval.shape, BF16), pltpu.SemaphoreType.DMA((2,))],
    )
    f_opp = send(f_send, flip_x)

    c_next = send(c_own, step_y(-1))
    a_far = send(a_prev, step_y(1))
    d_own = send(c_own, flip_core)
    b_prev = send(a_prev, flip_core)
    b_next = send(a_next, flip_core)
    c_prev = send(c_own, step_y(1))
    c_far = send(c_next, step_y(-1))
    d_next = send(c_next, flip_core)
    b_far = send(a_far, flip_core)
    d_prev = send(c_prev, flip_core)
    d_far = send(c_far, flip_core)

    own = attend(q_own, [f_own, b_own, c_own])
    opp = attend(q_opp, [a_prev, a_next, b_prev, b_next])
    opp = attend(q_opp, [a_own, b_own, d_own], opp)
    opp = attend(q_opp, [c_next, d_next], opp)
    opp = attend(q_opp, [a_far, c_prev, c_far], opp)
    o_send = attend(q_opp, [f_opp, b_far, d_prev, d_far], opp, True)
    rest = [a_prev, a_next, d_own, b_prev, b_next, c_next, d_next, a_far, b_far]
    rest += [c_prev, d_prev, c_far, d_far]
    o_own = attend(q_own, rest, own, True)
    o_other = send(o_send, flip_x)
    tail_args = [w_out, hidden_state, mod_gate, w_final.T, latent.T, step_row]
    advanced, mine, theirs = kernel(
        finish_kernel, [struct((64, BLK), F32), row, row], [o_own, o_other] + tail_args
    )

    route = []
    for w in range(window_devs):
        for f in range(frame_devs):
            to_w, to_f = (w + 1, f - half) if f >= half else (w - 1, f + half)
            if 0 <= to_w < window_devs:
                route.append((w * frame_devs + f, to_w * frame_devs + to_f))
    partner = lax.ppermute(advanced, ("win", "frm"), route)
    return (mine * advanced + theirs * partner).T


def solution(mesh):
    placed = (
        P(("win", "frm"), None),
        P(("win", "frm"), None),
        P(("win", "frm"), None),
        P("win", None),
        P("win", None),
        P("win", None),
        P(),
        P(),
        P(),
        P(),
        P("win"),
    )

    return jax.shard_map(
        on_device, mesh=mesh, in_specs=placed, out_specs=P(("win", "frm"), None), check_vma=False
    )
```

```python
import functools

import jax
import jax.numpy as jnp
from jax import lax
from jax.experimental import pallas as pl
from jax.experimental.pallas import tpu as pltpu
from jax.sharding import PartitionSpec as P

HEAD_DIM = 64
BLK = 256
D = 1536
HALF = 384
PAIRS = 3
LOG2E = 1.4426950408889634
F32 = jnp.float32
BF16 = jnp.bfloat16
VMEM = pl.BlockSpec(memory_space=pltpu.VMEM)
HBM = pl.BlockSpec(memory_space=pltpu.HBM)


def flip_x(i):
    return i ^ 8


def flip_core(i):
    return i ^ 1


def step_y(by):
    def to(i):
        x, y, c = i // 8, (i // 2) % 4, i % 2
        return x * 8 + ((y + by) % 4) * 2 + c

    return to


def send(value, to):
    return lax.ppermute(value, "frm", [(i, to(i)) for i in range(16)])


def kernel(body, out_shape, args, hbm=0, mib=16, **kw):
    many = isinstance(out_shape, list)
    cut = len(args) - hbm
    far = [pltpu.with_memory_space_constraint(a, pltpu.HBM) for a in args[cut:]]
    return pl.pallas_call(
        body,
        in_specs=[VMEM] * cut + [HBM] * hbm,
        out_specs=[VMEM] * len(out_shape) if many else VMEM,
        out_shape=out_shape,
        compiler_params=pltpu.CompilerParams(vmem_limit_bytes=mib << 20),
        **kw,
    )(*args[:cut], *far)


def struct(shape, dtype):
    return jax.ShapeDtypeStruct(shape, dtype)


def normalise(values):
    average = jnp.mean(values, axis=-1, keepdims=True)
    centred = values - average
    variance = jnp.mean(centred * centred, axis=-1, keepdims=True)
    return centred * lax.rsqrt(variance + 1e-06)


def upper():
    return lax.axis_index("frm") >= lax.axis_size("frm") // 2


def start_kernel(stale, a_own, a_send, sems):
    def halves(own):
        copies = []
        for i, (out, half) in enumerate([(a_send, 1 - own), (a_own, own)]):
            for j in range(2):
                cols = slice((2 * j + half) * HALF, (2 * j + half + 1) * HALF)
                to = out.at[:, j * HALF : (j + 1) * HALF]
                copies.append(pltpu.make_async_copy(stale.at[:, cols], to, sems.at[2 * i + j]))
        for c in copies:
            c.start()
        for c in copies:
            c.wait()

    @pl.when(upper())
    def _():
        halves(1)

    @pl.when(jnp.logical_not(upper()))
    def _():
        halves(0)


def query_kernel(*refs):
    sources, (q_send, q_own, modulated), buffers, sems = refs[:4], refs[4:7], refs[7:11], refs[11]
    hidden, shift, scale, w = buffers
    copies = [
        pltpu.make_async_copy(source, buffer, sems.at[i])
        for i, (source, buffer) in enumerate(zip(sources, buffers))
    ]
    for c in copies:
        c.start()
    for c in copies[:3]:
        c.wait()
    x = normalise(hidden[...].astype(F32))
    modulated[...] = (x * (1.0 + scale[...]) + shift[...]).astype(BF16)
    copies[3].wait()
    q = jnp.dot(modulated[...], w[...], preferred_element_type=F32).astype(BF16)
    q = q * jnp.asarray(HEAD_DIM**-0.5, BF16)

    @pl.when(jnp.logical_not(upper()))
    def _():
        q_own[...], q_send[...] = q[:, :HALF], q[:, HALF:]

    @pl.when(upper())
    def _():
        q_send[...], q_own[...] = q[:, :HALF], q[:, HALF:]


def fresh_kernel(modulated, step, source, f_send, f_own, step_row, w, sems):
    step_row[...] = jnp.broadcast_to(step[...].reshape(1, 1), step_row.shape)
    spans = [slice(i * 2 * HALF, (i + 1) * 2 * HALF) for i in range(2)]
    copies = [
        pltpu.make_async_copy(source.at[:, cols], w.at[:, cols], sems.at[i])
        for i, cols in enumerate(spans)
    ]
    for c in copies:
        c.start()
    for i, cols in enumerate(spans):
        copies[i].wait()
        x = jnp.dot(modulated[...], w[:, cols], preferred_element_type=F32).astype(BF16)
        to = slice(i * HALF, (i + 1) * HALF)

        @pl.when(jnp.logical_not(upper()))
        def _():
            f_own[:, to], f_send[:, to] = x[:, :HALF], x[:, HALF:]

        @pl.when(upper())
        def _():
            f_send[:, to], f_own[:, to] = x[:, :HALF], x[:, HALF:]


def attend_kernel(q_ref, *refs, n_keys, first, last):
    kvs, rest = refs[:n_keys], refs[n_keys:]
    if not first:
        acc_in, max_in = rest[0], rest[1]
        rest = rest[2:]
    lower = lax.broadcasted_iota(jnp.int32, (BLK, 128), 1) < HEAD_DIM
    for p in range(PAIRS):
        k_cols = slice(p * 128, (p + 1) * 128)
        v_cols = slice(HALF + p * 128, HALF + (p + 1) * 128)
        q = q_ref[:, k_cols]
        accs, tops = [], []
        for h, mine in enumerate((lower, jnp.logical_not(lower))):
            qh = jnp.where(mine, q, jnp.zeros_like(q))
            acc = top = None
            if not first:
                acc = acc_in[2 * p + h]
                top = jnp.where(mine, max_in[p], -3.0e38)
                top = jnp.max(top, axis=-1, keepdims=True)
            for kv in kvs:
                s = lax.dot_general(
                    qh, kv[:, k_cols], (((1,), (1,)), ((), ())), preferred_element_type=F32
                )
                new = jnp.max(s, axis=-1, keepdims=True)
                if top is not None:
                    new = jnp.maximum(top, new)
                probs = jnp.exp2((s - new) * LOG2E).astype(BF16)
                v = kv[:, v_cols]
                v = jnp.where(mine, v, jnp.ones_like(v))
                o = jnp.dot(probs, v, preferred_element_type=F32)
                acc = o if top is None else acc * jnp.exp2((top - new) * LOG2E) + o
                top = new
            accs.append(acc)
            tops.append(top)
        if last:
            summed = jnp.where(lower, accs[0], accs[1])
            total = pltpu.roll(jnp.where(lower, accs[1], accs[0]), HEAD_DIM, 1)
            rest[0][:, k_cols] = (summed / total).astype(BF16)
        else:
            rest[0][2 * p], rest[0][2 * p + 1] = accs
            rest[1][p] = jnp.where(lower, tops[0], tops[1])


def attend(q, arrays, state=None, last=False):
    args = [q, *arrays, *(state or ())]
    kw = {}
    if last:
        out_shape = struct((BLK, HALF), BF16)
    else:
        out_shape = [
            struct((2 * PAIRS, BLK, 128), F32),
            struct((PAIRS, BLK, 128), F32),
        ]
        if state:
            kw["input_output_aliases"] = {len(args) - 2: 0, len(args) - 1: 1}
    body = functools.partial(
        attend_kernel, n_keys=len(arrays), first=not state, last=last
    )
    return kernel(body, out_shape, args, **kw)


def finish_kernel(
    o_own,
    o_other,
    w_out,
    hidden,
    gate,
    w_final,
    latent,
    step,
    advanced,
    passed,
    mine,
    theirs,
):
    frames, windows = lax.axis_size("frm"), lax.axis_size("win")
    half = frames // 2
    frame, window = lax.axis_index("frm"), lax.axis_index("win")
    tail = frame >= half
    begin = jnp.where(tail, frame - half, frame) * BLK
    pos = (begin + lax.broadcasted_iota(jnp.int32, (1, BLK), 1)).astype(F32)
    ramp = (pos + 0.5) / (BLK * half)
    met = jnp.where(tail, window < windows - 1, window > 0)
    mine[...] = jnp.where(met, jnp.where(tail, 1.0 - ramp, ramp), 1.0)
    theirs[...] = jnp.where(met, jnp.where(tail, ramp, 1.0 - ramp), 0.0)

    own = pl.multiple_of(jnp.where(tail, HALF, 0), HALF)
    other = pl.multiple_of(HALF - own, HALF)
    mixed = jnp.dot(o_own[...], w_out[pl.ds(own, HALF), :], preferred_element_type=F32)
    mixed += jnp.dot(
        o_other[...], w_out[pl.ds(other, HALF), :], preferred_element_type=F32
    )
    combined = hidden[...].astype(F32) + gate[...] * mixed
    normed = normalise(combined).astype(BF16)
    velocity = lax.dot_general(
        w_final[...], normed, (((1,), (1,)), ((), ())), preferred_element_type=F32
    )
    result = latent[...] + step[...] * velocity
    advanced[...] = result
    passed[...] = result.astype(BF16)


def on_device(
    hidden_state,
    latent,
    stale_kv,
    mod_shift,
    mod_scale,
    mod_gate,
    w_query,
    w_keyval,
    w_out,
    w_final,
    step_size,
):
    frame_devs = lax.axis_size("frm")
    window_devs = lax.axis_size("win")
    half = frame_devs // 2
    half_kv = struct((BLK, 2 * HALF), BF16)
    half_q = struct((BLK, HALF), BF16)
    row = struct((1, BLK), F32)

    a_own, a_send = kernel(
        start_kernel,
        [half_kv, half_kv],
        [stale_kv],
        hbm=1,
        scratch_shapes=[pltpu.SemaphoreType.DMA((4,))],
    )
    c_own = send(a_send, flip_x)
    a_prev = send(a_own, step_y(1))
    a_next = send(a_own, step_y(-1))
    b_own = send(a_own, flip_core)

    q_send, q_own, modulated = kernel(
        query_kernel,
        [half_q, half_q, struct((BLK, D), BF16)],
        [hidden_state, mod_shift, mod_scale, w_query],
        hbm=4,
        scratch_shapes=[
            pltpu.VMEM((BLK, D), BF16),
            pltpu.VMEM((1, D), F32),
            pltpu.VMEM((1, D), F32),
            pltpu.VMEM(w_query.shape, BF16),
            pltpu.SemaphoreType.DMA((4,)),
        ],
    )
    q_opp = send(q_send, flip_x)
    f_send, f_own, step_row = kernel(
        fresh_kernel,
        [half_kv, half_kv, row],
        [modulated, step_size, w_keyval],
        hbm=1,
        scratch_shapes=[pltpu.VMEM(w_keyval.shape, BF16), pltpu.SemaphoreType.DMA((2,))],
    )
    f_opp = send(f_send, flip_x)

    c_next = send(c_own, step_y(-1))
    a_far = send(a_prev, step_y(1))
    d_own = send(c_own, flip_core)
    b_prev = send(a_prev, flip_core)
    b_next = send(a_next, flip_core)
    c_prev = send(c_own, step_y(1))
    c_far = send(c_next, step_y(-1))
    d_next = send(c_next, flip_core)
    b_far = send(a_far, flip_core)
    d_prev = send(c_prev, flip_core)
    d_far = send(c_far, flip_core)

    own = attend(q_own, [f_own, b_own, c_own])
    opp = attend(q_opp, [a_prev, a_next, b_prev, b_next])
    opp = attend(q_opp, [a_own, b_own, d_own], opp)
    opp = attend(q_opp, [c_next, d_next], opp)
    opp = attend(q_opp, [f_opp, a_far], opp)
    opp = attend(q_opp, [b_far, c_prev, d_prev, c_far], opp)
    o_send = attend(q_opp, [d_far], opp, True)
    rest = [a_prev, a_next, d_own, b_prev, b_next, c_next, d_next, a_far, b_far]
    rest += [c_prev, d_prev, c_far, d_far]
    o_own = attend(q_own, rest, own, True)
    o_other = send(o_send, flip_x)
    tail_args = [w_out, hidden_state, mod_gate, w_final.T, latent.T, step_row]
    advanced, passed, mine, theirs = kernel(
        finish_kernel,
        [struct((64, BLK), F32), struct((64, BLK), BF16), row, row],
        [o_own, o_other] + tail_args,
    )

    route = []
    for w in range(window_devs):
        for f in range(frame_devs):
            to_w, to_f = (w + 1, f - half) if f >= half else (w - 1, f + half)
            if 0 <= to_w < window_devs:
                route.append((w * frame_devs + f, to_w * frame_devs + to_f))
    partner = lax.ppermute(passed, ("win", "frm"), route)
    return (mine * advanced + theirs * partner).T


def solution(mesh):
    placed = (
        P(("win", "frm"), None),
        P(("win", "frm"), None),
        P(("win", "frm"), None),
        P("win", None),
        P("win", None),
        P("win", None),
        P(),
        P(),
        P(),
        P(),
        P("win"),
    )

    return jax.shard_map(
        on_device, mesh=mesh, in_specs=placed, out_specs=P(("win", "frm"), None), check_vma=False
    )
```
